512 devices in a mesh: stops: 256 (over y, x, z), veh: 2 (over core).
Axes of the slice: x: 4, y: 4, z: 16, core: 2. Of those that a mesh axis runs over, the one named last changes fastest.
Arguments:
- customer_features: bfloat16 [1048576, 128], P('stops'), may hold values from -20 to 20, as said below
- customer_loads: int32 [1048576], P('stops'), may hold values from 1 to 8
- truck_limits: int32 [2048], replicated, may hold values from 1536 to 3072
- truck_features: bfloat16 [2048, 128], replicated, may hold values from -20 to 20
- customer_average_matrix: bfloat16 [128, 128], replicated, may hold values from -1.5 to 1.5
- truck_identity_matrix: bfloat16 [128, 128], replicated, may hold values from -0.5 to 0.5
- hidden_offset: float32 [128], replicated, may hold values from -4 to 4
- output_projector: bfloat16 [128, 128], replicated, may hold values from -0.5 to 0.5
Outputs:
- new_vehicles: bfloat16 [2048, 128], P('veh')
The draws below stay inside these ranges and needn't reach their ends.
Inputs may be any that keep to these rules, and one draw needn't show every extreme that they name: `customer_features`: stop embeddings; stops of one block of 4096 form one region.
All inputs are finite; a program needn't handle non-finite values.
Results may differ from the reference program's by a relative error of at most 0.0085.
Values may be sent and summed in bfloat16 or wider, within the bound.
No kernel may reach another device: no remote copies, remote signals or barrier semaphores. Data moves between devices by JAX's collectives and lax.ppermute only.
A program may use at most 64 MiB of HBM per device.

```python
import jax
import jax.numpy as jnp
from jax import lax

STOP_DEV = 4096
FLEET_SIZE = 2048
K = 128
H = 128
STOPS = 1048576


def region_common(key):
    regions = STOPS // STOP_DEV
    centers = jax.random.normal(jax.random.fold_in(key, 7), (regions, K), jnp.float32)
    spread = jax.random.uniform(jax.random.fold_in(key, 8), (regions,), jnp.float32, 0.0, jnp.log(1.2))
    return centers * jnp.exp(spread)[:, None]


def noise_draw(key, shape):
    return jax.random.normal(key, shape, jnp.float32)


def truck_noise(key):
    noise = noise_draw(jax.random.fold_in(key, 17), (FLEET_SIZE, K))
    return noise


def draw_customer_features(key, part):
    centers = region_common(key)
    region = jnp.arange(STOPS) // STOP_DEV
    own_truck = truck_noise(key)
    preferred = jax.random.randint(jax.random.fold_in(key, 31), (STOPS,), 0, FLEET_SIZE)
    noise = noise_draw(jax.random.fold_in(key, 13), (STOPS, K))
    values = centers[region] + 0.7 * own_truck[preferred] + noise
    return jnp.clip(values, -20.0, 20.0).astype(jnp.bfloat16)


def draw_truck_features(key, part):
    centers = region_common(key)
    regions = STOPS // STOP_DEV
    home = jax.random.randint(jax.random.fold_in(key, 11), (FLEET_SIZE,), 0, regions)
    values = centers[home] + truck_noise(key)
    return jnp.clip(values, -20.0, 20.0).astype(jnp.bfloat16)


def with_ends(result, stream_key, least, largest):
    spot = [jax.random.randint(jax.random.fold_in(stream_key, axis), (), 0, length) for axis, length in enumerate(result.shape)]
    main_axis = result.shape.index(max(result.shape))
    next_to = spot[:main_axis] + [(spot[main_axis] + 1) % result.shape[main_axis]] + spot[main_axis + 1:]
    return result.at[tuple(spot)].set(least).at[tuple(next_to)].set(largest)


def centred(key, dims, width, limit, kind=jnp.bfloat16):
    drawn = width * jax.random.normal(key, dims, jnp.float32)
    return jnp.clip(drawn, min=-limit, max=limit).astype(kind)


def setup_inputs(seed: int = 0) -> dict:
    key_list = jax.random.split(jax.random.key(seed), 9)
    return {
        "customer_features": draw_customer_features(jax.random.fold_in(key_list[8], 71), 0),
        "customer_loads": with_ends(jax.random.randint(key_list[1], (STOPS,), 1, 9), jax.random.fold_in(key_list[1], 1), 1, 8).astype(jnp.int32),
        "truck_limits": with_ends(jax.random.randint(key_list[2], (FLEET_SIZE,), 1536, 3073), jax.random.fold_in(key_list[2], 1), 1536, 3072).astype(jnp.int32),
        "truck_features": draw_truck_features(jax.random.fold_in(key_list[8], 71), 0),
        "customer_average_matrix": centred(key_list[4], (K, H), (K // 8) ** -0.5, 1.5),
        "truck_identity_matrix": centred(key_list[5], (K, H), K ** -0.5, 0.5),
        "hidden_offset": centred(key_list[6], (H,), 1.0, 4.0, jnp.float32),
        "output_projector": centred(key_list[7], (H, K), H ** -0.5, 0.5),
    }


def log_sum(t):
    top = jnp.max(t, axis=1)
    return top + jnp.log(jnp.sum(jnp.exp(t - top[:, None]), axis=1))


def reference(customer_features, customer_loads, truck_limits, truck_features, customer_average_matrix, truck_identity_matrix, hidden_offset, output_projector):
    scale = 1.0 / (K ** 0.5)
    blocks = STOPS // STOP_DEV
    emb_blocks = customer_features.reshape(blocks, STOP_DEV, K)
    log_a = jnp.log(customer_loads.astype(jnp.float32)).reshape(blocks, STOP_DEV)
    target_share_logarithm = jnp.log(truck_limits.astype(jnp.float32))

    def first_pass(carry, item):
        emb, loga = item
        z = jnp.dot(emb, truck_features.T, preferred_element_type=jnp.float32) * scale
        first = loga - log_sum(z)
        return carry + jnp.sum(jnp.exp(first[:, None] + z), axis=0), None

    colsum, _ = lax.scan(first_pass, jnp.zeros((FLEET_SIZE,), jnp.float32), (emb_blocks, log_a))
    g_one = target_share_logarithm - jnp.log(colsum)

    def second_pass(carry, item):
        emb, loga = item
        z = jnp.dot(emb, truck_features.T, preferred_element_type=jnp.float32) * scale
        second = loga - log_sum(z + g_one[None, :])
        plan = jnp.exp(second[:, None] + g_one[None, :] + z).astype(jnp.bfloat16)
        den = jnp.sum(plan, axis=0, dtype=jnp.float32)
        num = jnp.dot(plan.T, emb, preferred_element_type=jnp.float32)
        return (carry[0] + num, carry[1] + den), None

    init = (jnp.zeros((FLEET_SIZE, K), jnp.float32), jnp.zeros((FLEET_SIZE,), jnp.float32))
    (num, den), _ = lax.scan(second_pass, init, (emb_blocks, log_a))
    centroid = (num / den[:, None]).astype(jnp.bfloat16)
    pre = jnp.dot(centroid, customer_average_matrix, preferred_element_type=jnp.float32)
    pre = pre + jnp.dot(truck_features, truck_identity_matrix, preferred_element_type=jnp.float32) + hidden_offset[None, :]
    hidden = jax.nn.silu(pre).astype(jnp.bfloat16)
    update = jnp.dot(hidden, output_projector, preferred_element_type=jnp.float32)
    return (truck_features.astype(jnp.float32) + update).astype(jnp.bfloat16)
```

```python
import jax
import jax.numpy as jnp
from jax import lax
from jax.experimental import pallas as pl
from jax.experimental.pallas import tpu as pltpu
from jax.sharding import Mesh, PartitionSpec as P

F32 = jnp.float32
BF16 = jnp.bfloat16
LANES = 128
BLOCK = 256
CHUNK = 256
LOG2E = 1.4426950408889634
ROW_BITS = 90.0
CAP_SCALE = 2.0**-20
WEIGHT_SCALE = 2.0**50


def on_lanes(column):
    n = column.shape[0] // LANES
    tiles = column.reshape(n, LANES, LANES)
    shape = (n, LANES, LANES)
    eye = lax.broadcasted_iota(jnp.int32, shape, 1) == lax.broadcasted_iota(jnp.int32, shape, 2)
    return jnp.sum(jnp.where(eye, tiles, 0.0), axis=1)


def row_of(ref, first, width):
    return jnp.concatenate(
        [ref[pl.ds(first + i, 1), :] for i in range(width // LANES)], axis=1
    )


def first_kernel(half_ref, veh_ref, stop_ref, load_ref, e_ref, out_ref, z_ref, col_ref):
    step = pl.program_id(0)
    vehicles, width = veh_ref.shape
    scale = LOG2E / width**0.5

    @pl.when(step == 0)
    def _():
        col_ref[...] = jnp.zeros_like(col_ref)

    stops = stop_ref[...]
    top = jnp.full((8, BLOCK), -jnp.inf, F32)
    for c in range(vehicles // CHUNK):
        rows = pl.ds(c * CHUNK, CHUNK)
        z = lax.dot_general(
            veh_ref[rows, :], stops, (((1,), (1,)), ((), ())), preferred_element_type=F32
        )
        z_ref[rows, :] = z
        top = jnp.maximum(top, jnp.max(z.reshape(CHUNK // 8, 8, BLOCK), axis=0))
    top = jnp.max(top, axis=0, keepdims=True) - ROW_BITS / scale
    total = jnp.zeros((8, BLOCK), F32)
    for c in range(vehicles // CHUNK):
        rows = pl.ds(c * CHUNK, CHUNK)
        e = jnp.exp2((z_ref[rows, :] - top) * scale)
        total = total + jnp.sum(e.reshape(CHUNK // 8, 8, BLOCK), axis=0)
        e_ref[0, rows, :] = e.astype(BF16)
    total = jnp.sum(total, axis=0, keepdims=True)
    first = half_ref[0] * (load_ref.shape[0] // 2) + step * (BLOCK // LANES)
    loads = row_of(load_ref, first, BLOCK).astype(F32)
    share = jnp.broadcast_to((loads / total).astype(BF16), (LANES, BLOCK))
    for c in range(vehicles // CHUNK):
        rows = pl.ds(c * CHUNK, CHUNK)
        col_ref[rows, :] += lax.dot_general(
            e_ref[0, rows, :], share, (((1,), (1,)), ((), ())), preferred_element_type=F32
        )

    @pl.when(step == pl.num_programs(0) - 1)
    def _():
        col = on_lanes(col_ref[...]).astype(BF16)
        out_ref[...] = jnp.broadcast_to(col[None], out_ref.shape)


def first_pass(half, veh, stops, loads, peers):
    vehicles, width = veh.shape
    blocks = stops.shape[0] // 2 // BLOCK
    return pl.pallas_call(
        first_kernel,
        grid_spec=pltpu.PrefetchScalarGridSpec(
            num_scalar_prefetch=1,
            grid=(blocks,),
            in_specs=[
                pl.BlockSpec((vehicles, width), lambda s, h: (0, 0)),
                pl.BlockSpec((BLOCK, width), lambda s, h: (h[0] * blocks + s, 0)),
                pl.BlockSpec(loads.shape, lambda s, h: (0, 0)),
            ],
            out_specs=[
                pl.BlockSpec((1, vehicles, BLOCK), lambda s, h: (s, 0, 0)),
                pl.BlockSpec((peers, vehicles // LANES, LANES), lambda s, h: (0, 0, 0)),
            ],
            scratch_shapes=[
                pltpu.VMEM((vehicles, BLOCK), F32),
                pltpu.VMEM((vehicles, LANES), F32),
            ],
        ),
        out_shape=[
            jax.ShapeDtypeStruct((blocks, vehicles, BLOCK), BF16),
            jax.ShapeDtypeStruct((peers, vehicles // LANES, LANES), BF16),
        ],
        compiler_params=pltpu.CompilerParams(vmem_limit_bytes=32 << 20),
        name="first_pass",
    )(half, veh, stops, loads)


def sum_and_copy_kernel(in_ref, out_ref):
    total = jnp.sum(in_ref[...].astype(F32), axis=0)
    out_ref[...] = jnp.broadcast_to(total.astype(out_ref.dtype)[None], out_ref.shape)


def sum_and_copy(parts, copies):
    return pl.pallas_call(
        sum_and_copy_kernel,
        out_shape=jax.ShapeDtypeStruct((copies,) + parts.shape[1:], parts.dtype),
        name="sum_and_copy",
    )(parts)


def second_kernel(half_ref, cap_ref, part_ref, load_ref, stop_ref, e_ref, out_ref, g_ref, num_ref):
    step = pl.program_id(0)
    vehicles = num_ref.shape[0]

    @pl.when(step == 0)
    def _():
        num_ref[...] = jnp.zeros_like(num_ref)
        colsum = jnp.sum(part_ref[...].astype(F32), axis=0)
        g = (cap_ref[...].astype(F32) * CAP_SCALE) / colsum
        shape = (LANES, LANES)
        eye = lax.broadcasted_iota(jnp.int32, shape, 0) == lax.broadcasted_iota(jnp.int32, shape, 1)
        for r in range(vehicles // LANES):
            spread = jnp.where(eye, jnp.broadcast_to(g[r : r + 1], shape), 0.0)
            column = jnp.sum(spread, axis=1, keepdims=True)
            g_ref[pl.ds(r * LANES, LANES), :] = jnp.broadcast_to(column, shape)

    total = jnp.zeros((8, BLOCK), F32)
    for c in range(vehicles // CHUNK):
        rows = pl.ds(c * CHUNK, CHUNK)
        g = g_ref[rows, :]
        t = e_ref[0, rows, :].astype(F32) * jnp.concatenate([g] * (BLOCK // LANES), axis=1)
        total = total + jnp.sum(t.reshape(CHUNK // 8, 8, BLOCK), axis=0)
    total = jnp.sum(total, axis=0, keepdims=True)
    first = half_ref[0] * (load_ref.shape[0] // 2) + step * (BLOCK // LANES)
    loads = row_of(load_ref, first, BLOCK).astype(F32)
    weight = (loads * WEIGHT_SCALE / total).astype(BF16).astype(F32)
    scaled = stop_ref[...].astype(F32).T * weight
    right = jnp.concatenate(
        [scaled.astype(BF16), jnp.broadcast_to(weight.astype(BF16), (LANES, BLOCK))], axis=0
    )
    for c in range(vehicles // CHUNK):
        rows = pl.ds(c * CHUNK, CHUNK)
        num_ref[rows, :] += lax.dot_general(
            e_ref[0, rows, :], right, (((1,), (1,)), ((), ())), preferred_element_type=F32
        )

    @pl.when(step == pl.num_programs(0) - 1)
    def _():
        peers, tall, width = out_ref.shape
        own = vehicles // peers
        half = peers // 2
        shape = (own, LANES)
        eye = lax.broadcasted_iota(jnp.int32, shape, 0) == lax.broadcasted_iota(jnp.int32, shape, 1)
        line = lax.broadcasted_iota(jnp.int32, (tall - own, LANES), 0)
        for v in range(2):
            for r in range(half):
                rows = pl.ds((v * half + r) * own, own)
                out_ref[r * 2 + v, 0:own, :] = num_ref[rows, 0:width].astype(BF16)
                den = jnp.sum(jnp.where(eye, num_ref[rows, width:], 0.0), axis=0, keepdims=True)
                high = den.astype(BF16).astype(F32)
                tail = jnp.where(line == 0, high, jnp.where(line == 1, den - high, 0.0))
                out_ref[r * 2 + v, own:tall, :] = tail.astype(BF16)


def second_pass(half, caps, parts, loads, stops, e, peers):
    blocks, vehicles, _ = e.shape
    width = stops.shape[1]
    tall = vehicles // peers + 8
    return pl.pallas_call(
        second_kernel,
        grid_spec=pltpu.PrefetchScalarGridSpec(
            num_scalar_prefetch=1,
            grid=(blocks,),
            in_specs=[
                pl.BlockSpec(caps.shape, lambda s, h: (0, 0)),
                pl.BlockSpec(parts.shape, lambda s, h: (0, 0, 0)),
                pl.BlockSpec(loads.shape, lambda s, h: (0, 0)),
                pl.BlockSpec((BLOCK, width), lambda s, h: (h[0] * blocks + s, 0)),
                pl.BlockSpec((1, vehicles, BLOCK), lambda s, h: (s, 0, 0)),
            ],
            out_specs=pl.BlockSpec((peers, tall, width), lambda s, h: (0, 0, 0)),
            scratch_shapes=[
                pltpu.VMEM((vehicles, LANES), F32),
                pltpu.VMEM((vehicles, width + LANES), F32),
            ],
        ),
        out_shape=jax.ShapeDtypeStruct((peers, tall, width), BF16),
        compiler_params=pltpu.CompilerParams(vmem_limit_bytes=32 << 20),
        name="second_pass",
    )(half, caps, parts, loads, stops, e)


def update_kernel(
    where_ref, part_ref, veh_ref, average_ref, identity_ref, offset_ref, projector_ref, out_ref
):
    own, width = veh_ref.shape
    total = jnp.sum(part_ref[...].astype(F32), axis=0)
    den = total[own : own + 1, :] + total[own + 1 : own + 2, :]
    shape = (own, LANES)
    eye = lax.broadcasted_iota(jnp.int32, shape, 0) == lax.broadcasted_iota(jnp.int32, shape, 1)
    den = jnp.sum(jnp.where(eye, jnp.broadcast_to(den, shape), 0.0), axis=1, keepdims=True)
    centroid = (total[0:own] / den).astype(BF16)
    rows = veh_ref[...]
    pre = jnp.dot(centroid, average_ref[...], preferred_element_type=F32)
    pre = pre + jnp.dot(rows, identity_ref[...], preferred_element_type=F32) + offset_ref[...]
    hidden = jax.nn.silu(pre).astype(BF16)
    update = jnp.dot(hidden, projector_ref[...], preferred_element_type=F32)
    new = (rows.astype(F32) + update).astype(BF16)
    out_ref[...] = jnp.broadcast_to(new[None], out_ref.shape)


def update_rows(where, parts, veh, average, identity, offset, projector, copies, own):
    width = veh.shape[1]
    whole = lambda s, w: (0, 0)
    return pl.pallas_call(
        update_kernel,
        grid_spec=pltpu.PrefetchScalarGridSpec(
            num_scalar_prefetch=1,
            grid=(1,),
            in_specs=[
                pl.BlockSpec(parts.shape, lambda s, w: (0, 0, 0)),
                pl.BlockSpec((own, width), lambda s, w: (w[0], 0)),
                pl.BlockSpec(average.shape, whole),
                pl.BlockSpec(identity.shape, whole),
                pl.BlockSpec(offset.shape, whole),
                pl.BlockSpec(projector.shape, whole),
            ],
            out_specs=pl.BlockSpec((copies, own, width), lambda s, w: (0, 0, 0)),
        ),
        out_shape=jax.ShapeDtypeStruct((copies, own, width), BF16),
        name="update_rows",
    )(where, parts, veh, average, identity, offset, projector)


def swap(array, axes):
    return lax.all_to_all(array, axes, 0, 0, tiled=True)


def solution(mesh):
    stops_n = mesh.shape["stops"]
    y = x = 4
    pair = 2
    far = stops_n // (y * x * pair)
    inner = Mesh(
        mesh.devices.reshape(y, x, far, pair, mesh.shape["veh"]), ("y", "x", "far", "pair", "veh")
    )

    def on_device(
        customer_features,
        customer_loads,
        truck_limits,
        truck_features,
        customer_average_matrix,
        truck_identity_matrix,
        hidden_offset,
        output_projector,
    ):
        vehicles, width = truck_features.shape
        core = lax.axis_index("veh")
        half = core.astype(jnp.int32).reshape(1)
        near = (lax.axis_index("y") * x + lax.axis_index("x")) * pair + lax.axis_index("pair")
        chips = y * x * pair
        where = (core * chips + near).astype(jnp.int32).reshape(1)
        loads = customer_loads.reshape(-1, LANES)
        caps = truck_limits.reshape(-1, LANES)

        e, col = first_pass(half, truck_features, customer_features, loads, y * x * 2)
        col = swap(col, ("y", "x", "veh"))
        col = swap(sum_and_copy(col, far * pair), ("far", "pair"))
        parts = second_pass(half, caps, col, loads, customer_features, e, chips * 2)
        parts = swap(parts, ("y", "x", "pair", "veh"))
        parts = swap(sum_and_copy(parts, far), "far")
        new = update_rows(
            where,
            parts,
            truck_features,
            customer_average_matrix,
            truck_identity_matrix,
            hidden_offset.reshape(1, -1),
            output_projector,
            chips,
            vehicles // (chips * 2),
        )
        new = swap(new, ("y", "x", "pair"))
        return new.reshape(-1, width)

    split = ("y", "x", "far", "pair")
    placed = (P(split, None), P(split), P(), P(), P(), P(), P(), P())
    return jax.shard_map(
        on_device, mesh=inner, in_specs=placed, out_specs=P("veh", None), check_vma=False
    )
```

```python
import jax
import jax.numpy as jnp
from jax import lax
from jax.experimental import pallas as pl
from jax.experimental.pallas import tpu as pltpu
from jax.sharding import Mesh, PartitionSpec as P

F32 = jnp.float32
BF16 = jnp.bfloat16
LANES = 128
BLOCK = 256
CHUNK = 256
TALL = 512
LOG2E = 1.4426950408889634
ROW_BITS = 90.0
CAP_SCALE = 2.0**-20
WEIGHT_SCALE = 2.0**50
FIRST_LIMIT = 48 << 20
SECOND_LIMIT = 16 << 20
SMALL_LIMIT = 4 << 20
LAST_DIMS = (((1,), (1,)), ((), ()))
VMEM = pl.BlockSpec(memory_space=pltpu.VMEM)
SMEM = pl.BlockSpec(memory_space=pltpu.SMEM)
ANY = pl.BlockSpec(memory_space=pl.ANY)


def diagonal(shape):
    n = len(shape)
    return lax.broadcasted_iota(jnp.int32, shape, n - 2) == lax.broadcasted_iota(
        jnp.int32, shape, n - 1
    )


def on_lanes(column):
    shape = (column.shape[0] // LANES, LANES, LANES)
    return jnp.sum(jnp.where(diagonal(shape), column.reshape(shape), 0.0), axis=1)


def loads_of(ref, b):
    n = BLOCK // LANES
    return jnp.concatenate([ref[pl.ds(b * n + i, 1), :] for i in range(n)], axis=1).astype(F32)


def first_kernel(
    half_ref,
    veh_hbm,
    stop_hbm,
    load_hbm,
    cap_hbm,
    e_ref,
    out_ref,
    turned_ref,
    int_ref,
    veh_ref,
    stop_ref,
    z0_ref,
    z1_ref,
    share_ref,
    sem,
):
    vehicles, width = veh_ref.shape
    scale = LOG2E / width**0.5
    blocks = e_ref.shape[0]
    chunks = vehicles // CHUNK
    own = blocks * BLOCK
    tall = own // LANES
    half = half_ref[0]
    z_refs = (z0_ref, z1_ref)
    mine = pl.ds(pl.multiple_of(half * own, own), own)
    lines = pl.ds(pl.multiple_of(half * tall, tall), tall)
    moves = [
        pltpu.make_async_copy(veh_hbm, veh_ref, sem.at[0]),
        pltpu.make_async_copy(stop_hbm.at[mine], stop_ref, sem.at[1]),
        pltpu.make_async_copy(load_hbm.at[lines], int_ref.at[pl.ds(0, tall)], sem.at[2]),
        pltpu.make_async_copy(cap_hbm, int_ref.at[pl.ds(tall, cap_hbm.shape[0])], sem.at[3]),
    ]
    for move in moves:
        move.start()
    for move in moves:
        move.wait()
    lowest = jnp.full((8, BLOCK), -jnp.inf, F32)

    def turn(b):
        turned = stop_ref[pl.ds(pl.multiple_of(b * BLOCK, BLOCK), BLOCK), :].T
        turned_ref[b] = turned
        return turned

    def scores(z_ref, turned, c, top):
        rows = pl.ds(c * CHUNK, CHUNK)
        z = jnp.dot(veh_ref[rows, :], turned, preferred_element_type=F32)
        z_ref[rows, :] = z
        return jnp.maximum(top, jnp.max(z.reshape(CHUNK // 8, 8, BLOCK), axis=0))

    def exponentials(b, z_ref, top, c, total):
        rows = pl.ds(c * CHUNK, CHUNK)
        e = jnp.exp2((z_ref[rows, :] - top) * scale)
        e_ref[b, rows, :] = e.astype(BF16)
        return total + jnp.sum(e.reshape(CHUNK // 8, 8, BLOCK), axis=0)

    def level(top):
        return jnp.max(top, axis=0, keepdims=True) - ROW_BITS / scale

    def step(b, slot, top, more):
        turned = turn(b + 1) if more else None
        after = lowest
        total = jnp.zeros((8, BLOCK), F32)
        for c in range(chunks):
            if more:
                after = scores(z_refs[1 - slot], turned, c, after)
            total = exponentials(b, z_refs[slot], top, c, total)
        total = jnp.sum(total, axis=0, keepdims=True)
        share = (loads_of(int_ref, b) / total).astype(BF16)
        share_ref[b] = jnp.broadcast_to(share, (LANES, BLOCK))
        return level(after)

    turned = turn(0)
    top = lowest
    for c in range(chunks):
        top = scores(z_refs[0], turned, c, top)
    top = level(top)

    def two(p, top):
        return step(2 * p + 1, 1, step(2 * p, 0, top, True), True)

    top = lax.fori_loop(0, blocks // 2 - 1, two, top)
    top = step(blocks - 2, 0, top, True)
    step(blocks - 1, 1, top, False)

    n = TALL // LANES
    for k in range(vehicles // TALL):
        rows = pl.ds(k * TALL, TALL)
        col = sum(
            lax.dot_general(
                e_ref[b, rows, :], share_ref[b], LAST_DIMS, preferred_element_type=F32
            )
            for b in range(blocks)
        )
        col = on_lanes(col).astype(out_ref.dtype)
        out_ref[:, k * n : (k + 1) * n, :] = jnp.broadcast_to(
            col[None], (out_ref.shape[0], n, LANES)
        )


def first_pass(half, veh, stops, loads, caps, peers):
    vehicles, width = veh.shape
    blocks = stops.shape[0] // 2 // BLOCK
    return pl.pallas_call(
        first_kernel,
        in_specs=[SMEM, ANY, ANY, ANY, ANY],
        out_specs=[VMEM, VMEM, VMEM, VMEM],
        out_shape=[
            pltpu.VMEM((blocks, vehicles, BLOCK), BF16),
            pltpu.VMEM((peers, vehicles // LANES, LANES), BF16),
            pltpu.VMEM((blocks, width, BLOCK), BF16),
            pltpu.VMEM((loads.shape[0] // 2 + caps.shape[0], LANES), jnp.int32),
        ],
        scratch_shapes=[
            pltpu.VMEM((vehicles, width), BF16),
            pltpu.VMEM((blocks * BLOCK, width), BF16),
            pltpu.VMEM((vehicles, BLOCK), F32),
            pltpu.VMEM((vehicles, BLOCK), F32),
            pltpu.VMEM((blocks, LANES, BLOCK), BF16),
            pltpu.SemaphoreType.DMA((4,)),
        ],
        compiler_params=pltpu.CompilerParams(vmem_limit_bytes=FIRST_LIMIT),
        name="first_pass",
    )(half, veh, stops, loads, caps)


def sum_and_copy_kernel(in_ref, out_ref):
    total = jnp.sum(in_ref[...].astype(F32), axis=0)
    out_ref[...] = jnp.broadcast_to(total.astype(out_ref.dtype)[None], out_ref.shape)


def sum_and_copy(parts, copies):
    return pl.pallas_call(
        sum_and_copy_kernel,
        in_specs=[VMEM],
        out_specs=VMEM,
        out_shape=jax.ShapeDtypeStruct((copies,) + parts.shape[1:], parts.dtype),
        compiler_params=pltpu.CompilerParams(vmem_limit_bytes=SMALL_LIMIT),
        name="sum_and_copy",
    )(parts)


def second_kernel(part_ref, turned_ref, int_ref, e_ref, out_ref, g_ref, right_ref):
    blocks, vehicles, _ = e_ref.shape
    width = turned_ref.shape[1]
    lines = vehicles // LANES
    tall = int_ref.shape[0] - lines
    colsum = jnp.sum(part_ref[...].astype(F32), axis=0)
    g = (int_ref[tall:, :].astype(F32) * CAP_SCALE) / colsum
    square = (LANES, LANES)
    eye = diagonal(square)
    for r in range(lines):
        spread = jnp.where(eye, jnp.broadcast_to(g[r : r + 1], square), 0.0)
        column = jnp.sum(spread, axis=1, keepdims=True)
        g_ref[pl.ds(r * LANES, LANES), :] = jnp.broadcast_to(column, square)

    def weigh(b, _):
        total = jnp.zeros((8, BLOCK), F32)
        for c in range(vehicles // CHUNK):
            rows = pl.ds(c * CHUNK, CHUNK)
            g = jnp.concatenate([g_ref[rows, :]] * (BLOCK // LANES), axis=1)
            t = e_ref[b, rows, :].astype(F32) * g
            total = total + jnp.sum(t.reshape(CHUNK // 8, 8, BLOCK), axis=0)
        total = jnp.sum(total, axis=0, keepdims=True)
        weight = (loads_of(int_ref, b) * WEIGHT_SCALE / total).astype(BF16)
        right_ref[b, 0:width, :] = (turned_ref[b].astype(F32) * weight.astype(F32)).astype(BF16)
        right_ref[b, width:, :] = jnp.broadcast_to(weight, (LANES, BLOCK))
        return 0

    lax.fori_loop(0, blocks, weigh, 0)
    peers, own_tall, _ = out_ref.shape
    own = vehicles // peers
    half = peers // 2
    eye = diagonal((own, LANES))
    line = lax.broadcasted_iota(jnp.int32, (own_tall - own, LANES), 0)
    for k in range(vehicles // TALL):
        rows = pl.ds(k * TALL, TALL)
        num = sum(
            lax.dot_general(
                e_ref[b, rows, :], right_ref[b], LAST_DIMS, preferred_element_type=F32
            )
            for b in range(blocks)
        )
        for q in range(TALL // own):
            r = k * (TALL // own) + q
            to = (r % half) * 2 + r // half
            mine = num[q * own : (q + 1) * own]
            out_ref[to, 0:own, :] = mine[:, 0:width].astype(BF16)
            den = jnp.sum(jnp.where(eye, mine[:, width:], 0.0), axis=0, keepdims=True)
            high = den.astype(BF16).astype(F32)
            tail = jnp.where(line == 0, high, jnp.where(line == 1, den - high, 0.0))
            out_ref[to, own:own_tall, :] = tail.astype(BF16)


def second_pass(parts, turned, ints, e, peers):
    blocks, vehicles, _ = e.shape
    width = turned.shape[1]
    return pl.pallas_call(
        second_kernel,
        in_specs=[VMEM, VMEM, VMEM, VMEM],
        out_specs=VMEM,
        out_shape=jax.ShapeDtypeStruct((peers, vehicles // peers + 8, width), BF16),
        scratch_shapes=[
            pltpu.VMEM((vehicles, LANES), F32),
            pltpu.VMEM((blocks, width + LANES, BLOCK), BF16),
        ],
        compiler_params=pltpu.CompilerParams(vmem_limit_bytes=SECOND_LIMIT),
        name="second_pass",
    )(parts, turned, ints, e)


def update_kernel(
    where_ref, part_ref, veh_ref, average_ref, identity_ref, offset_ref, projector_ref, out_ref
):
    own = part_ref.shape[1] - 8
    total = jnp.sum(part_ref[...].astype(F32), axis=0)
    den = total[own : own + 1, :] + total[own + 1 : own + 2, :]
    shape = (own, LANES)
    spread = jnp.where(diagonal(shape), jnp.broadcast_to(den, shape), 0.0)
    den = jnp.sum(spread, axis=1, keepdims=True)
    centroid = (total[0:own] / den).astype(BF16)
    rows = veh_ref[pl.ds(pl.multiple_of(where_ref[0] * own, own), own), :]
    pre = jnp.dot(centroid, average_ref[...], preferred_element_type=F32)
    pre = pre + jnp.dot(rows, identity_ref[...], preferred_element_type=F32) + offset_ref[...]
    hidden = jax.nn.silu(pre).astype(BF16)
    update = jnp.dot(hidden, projector_ref[...], preferred_element_type=F32)
    new = (rows.astype(F32) + update).astype(BF16)
    for r in range(out_ref.shape[0] // own):
        out_ref[pl.ds(r * own, own), :] = new


def update_rows(where, parts, veh, average, identity, offset, projector, copies):
    own = parts.shape[1] - 8
    return pl.pallas_call(
        update_kernel,
        in_specs=[SMEM] + [VMEM] * 6,
        out_specs=VMEM,
        out_shape=jax.ShapeDtypeStruct((copies * own, veh.shape[1]), BF16),
        compiler_params=pltpu.CompilerParams(vmem_limit_bytes=SMALL_LIMIT),
        name="update_rows",
    )(where, parts, veh, average, identity, offset, projector)


def swap(array, axes):
    return lax.all_to_all(array, axes, 0, 0, tiled=True)


def solution(mesh):
    stops_n = mesh.shape["stops"]
    y = x = 4
    pair = 2
    far = stops_n // (y * x * pair)
    inner = Mesh(
        mesh.devices.reshape(y, x, far, pair, mesh.shape["veh"]), ("y", "x", "far", "pair", "veh")
    )

    def on_device(
        customer_features,
        customer_loads,
        truck_limits,
        truck_features,
        customer_average_matrix,
        truck_identity_matrix,
        hidden_offset,
        output_projector,
    ):
        core = lax.axis_index("veh")
        half = core.astype(jnp.int32).reshape(1)
        near = (lax.axis_index("y") * x + lax.axis_index("x")) * pair + lax.axis_index("pair")
        chips = y * x * pair
        where = (core * chips + near).astype(jnp.int32).reshape(1)
        loads = customer_loads.reshape(-1, LANES)
        caps = truck_limits.reshape(-1, LANES)

        e, col, turned, ints = first_pass(
            half, truck_features, customer_features, loads, caps, y * x * 2
        )
        col = swap(col, ("y", "x", "veh"))
        col = swap(sum_and_copy(col, far * pair), ("far", "pair"))
        parts = second_pass(col, turned, ints, e, chips * 2)
        parts = swap(parts, ("y", "x", "pair", "veh"))
        parts = swap(sum_and_copy(parts, far), "far")
        new = update_rows(
            where,
            parts,
            truck_features,
            customer_average_matrix,
            truck_identity_matrix,
            hidden_offset.reshape(1, -1),
            output_projector,
            chips,
        )
        return swap(new, ("y", "x", "pair"))

    split = ("y", "x", "far", "pair")
    placed = (P(split, None), P(split), P(), P(), P(), P(), P(), P())
    return jax.shard_map(
        on_device, mesh=inner, in_specs=placed, out_specs=P("veh", None), check_vma=False
    )
```

```python
import functools

import jax
import jax.numpy as jnp
from jax import lax
from jax.experimental import pallas as pl
from jax.experimental.pallas import tpu as pltpu
from jax.sharding import Mesh, PartitionSpec as P

F32 = jnp.float32
BF16 = jnp.bfloat16
LANES = 128
BLOCK = 256
CHUNK = 256
TALL = 512
LOG2E = 1.4426950408889634
ROW_BITS = 90.0
CAP_SCALE = 2.0**-20
WEIGHT_SCALE = 2.0**50
FIRST_LIMIT = 48 << 20
SECOND_LIMIT = 16 << 20
SMALL_LIMIT = 4 << 20
LAST_DIMS = (((1,), (1,)), ((), ()))
VMEM = pl.BlockSpec(memory_space=pltpu.VMEM)
SMEM = pl.BlockSpec(memory_space=pltpu.SMEM)
ANY = pl.BlockSpec(memory_space=pl.ANY)


def diagonal(shape):
    n = len(shape)
    return lax.broadcasted_iota(jnp.int32, shape, n - 2) == lax.broadcasted_iota(
        jnp.int32, shape, n - 1
    )


def loads_of(ref, b):
    n = BLOCK // LANES
    return jnp.concatenate([ref[pl.ds(b * n + i, 1), :] for i in range(n)], axis=1).astype(F32)


def first_kernel(
    half_ref,
    veh_hbm,
    stop_hbm,
    load_hbm,
    cap_hbm,
    e_ref,
    out_ref,
    turned_ref,
    int_ref,
    veh_ref,
    stop_ref,
    z0_ref,
    z1_ref,
    share_ref,
    sem,
):
    vehicles, width = veh_ref.shape
    scale = LOG2E / width**0.5
    blocks = e_ref.shape[0]
    chunks = vehicles // CHUNK
    own = blocks * BLOCK
    tall = own // LANES
    half = half_ref[0]
    z_refs = (z0_ref, z1_ref)
    mine = pl.ds(pl.multiple_of(half * own, own), own)
    lines = pl.ds(pl.multiple_of(half * tall, tall), tall)
    moves = [
        pltpu.make_async_copy(veh_hbm, veh_ref, sem.at[0]),
        pltpu.make_async_copy(stop_hbm.at[mine], stop_ref, sem.at[1]),
        pltpu.make_async_copy(load_hbm.at[lines], int_ref.at[pl.ds(0, tall)], sem.at[2]),
        pltpu.make_async_copy(cap_hbm, int_ref.at[pl.ds(tall, cap_hbm.shape[0])], sem.at[3]),
    ]
    for move in moves:
        move.start()
    for move in moves:
        move.wait()
    lowest = jnp.full((8, BLOCK), -jnp.inf, F32)

    def turn(b):
        turned = stop_ref[pl.ds(pl.multiple_of(b * BLOCK, BLOCK), BLOCK), :].T
        turned_ref[b] = turned
        return turned

    def scores(z_ref, turned, c, top):
        rows = pl.ds(c * CHUNK, CHUNK)
        z = jnp.dot(veh_ref[rows, :], turned, preferred_element_type=F32)
        z_ref[rows, :] = z
        return jnp.maximum(top, jnp.max(z.reshape(CHUNK // 8, 8, BLOCK), axis=0))

    def exponentials(b, z_ref, top, c, total):
        rows = pl.ds(c * CHUNK, CHUNK)
        e = jnp.exp2((z_ref[rows, :] - top) * scale)
        e_ref[b, rows, :] = e.astype(BF16)
        return total + jnp.sum(e.reshape(CHUNK // 8, 8, BLOCK), axis=0)

    def level(top):
        return jnp.max(top, axis=0, keepdims=True) - ROW_BITS / scale

    def step(b, slot, top, more):
        turned = turn(b + 1) if more else None
        after = lowest
        total = jnp.zeros((8, BLOCK), F32)
        for c in range(chunks):
            if more:
                after = scores(z_refs[1 - slot], turned, c, after)
            total = exponentials(b, z_refs[slot], top, c, total)
        total = jnp.sum(total, axis=0, keepdims=True)
        share = (loads_of(int_ref, b) / total).astype(BF16)
        share_ref[b] = jnp.broadcast_to(share, (LANES, BLOCK))
        return level(after)

    turned = turn(0)
    top = lowest
    for c in range(chunks):
        top = scores(z_refs[0], turned, c, top)
    top = level(top)

    def two(p, top):
        return step(2 * p + 1, 1, step(2 * p, 0, top, True), True)

    top = lax.fori_loop(0, blocks // 2 - 1, two, top)
    top = step(blocks - 2, 0, top, True)
    step(blocks - 1, 1, top, False)

    for k in range(vehicles // LANES):
        rows = pl.ds(k * LANES, LANES)
        col = jnp.zeros((LANES, LANES), F32)
        for b in range(blocks):
            t = e_ref[b, rows, :] * share_ref[b]
            t = t[:, 0:LANES] + t[:, LANES:BLOCK]
            col = col + t.astype(F32)
        col = jnp.sum(col.T, axis=0, keepdims=True).astype(out_ref.dtype)
        out_ref[:, k : k + 1, :] = jnp.broadcast_to(col[None], (out_ref.shape[0], 1, LANES))


def first_pass(half, veh, stops, loads, caps, peers):
    vehicles, width = veh.shape
    blocks = stops.shape[0] // 2 // BLOCK
    return pl.pallas_call(
        first_kernel,
        in_specs=[SMEM, ANY, ANY, ANY, ANY],
        out_specs=[VMEM, VMEM, VMEM, VMEM],
        out_shape=[
            pltpu.VMEM((blocks, vehicles, BLOCK), BF16),
            pltpu.VMEM((peers, vehicles // LANES, LANES), BF16),
            pltpu.VMEM((blocks, width, BLOCK), BF16),
            pltpu.VMEM((loads.shape[0] // 2 + caps.shape[0], LANES), jnp.int32),
        ],
        scratch_shapes=[
            pltpu.VMEM((vehicles, width), BF16),
            pltpu.VMEM((blocks * BLOCK, width), BF16),
            pltpu.VMEM((vehicles, BLOCK), F32),
            pltpu.VMEM((vehicles, BLOCK), F32),
            pltpu.VMEM((blocks, LANES, BLOCK), BF16),
            pltpu.SemaphoreType.DMA((4,)),
        ],
        compiler_params=pltpu.CompilerParams(vmem_limit_bytes=FIRST_LIMIT),
        name="first_pass",
    )(half, veh, stops, loads, caps)


def sum_and_copy_kernel(in_ref, out_ref):
    total = jnp.sum(in_ref[...].astype(F32), axis=0)
    out_ref[...] = jnp.broadcast_to(total.astype(out_ref.dtype)[None], out_ref.shape)


def sum_and_copy(parts, copies):
    return pl.pallas_call(
        sum_and_copy_kernel,
        in_specs=[VMEM],
        out_specs=VMEM,
        out_shape=jax.ShapeDtypeStruct((copies,) + parts.shape[1:], parts.dtype),
        compiler_params=pltpu.CompilerParams(vmem_limit_bytes=SMALL_LIMIT),
        name="sum_and_copy",
    )(parts)


def second_kernel(part_ref, turned_ref, int_ref, e_ref, out_ref, g_ref, right_ref):
    blocks, vehicles, _ = e_ref.shape
    width = turned_ref.shape[1]
    lines = vehicles // LANES
    tall = int_ref.shape[0] - lines
    colsum = jnp.sum(part_ref[...].astype(F32), axis=0)
    g = (int_ref[tall:, :].astype(F32) * CAP_SCALE) / colsum
    square = (LANES, LANES)
    eye = diagonal(square)
    for r in range(lines):
        spread = jnp.where(eye, jnp.broadcast_to(g[r : r + 1], square), 0.0)
        column = jnp.sum(spread, axis=1, keepdims=True)
        g_ref[pl.ds(r * LANES, LANES), :] = jnp.broadcast_to(column, square).astype(BF16)

    for b in range(blocks):
        total = jnp.zeros((16, BLOCK), F32)
        for c in range(vehicles // CHUNK):
            rows = pl.ds(c * CHUNK, CHUNK)
            g = jnp.concatenate([g_ref[rows, :]] * (BLOCK // LANES), axis=1)
            t = (e_ref[b, rows, :] * g).reshape(CHUNK // 32, 2, 16, BLOCK)
            t = (t[:, 0] + t[:, 1]).astype(F32)
            total = total + jnp.sum(t, axis=0)
        total = jnp.sum(total, axis=0, keepdims=True)
        weight = (loads_of(int_ref, b) * WEIGHT_SCALE / total).astype(BF16)
        right_ref[b, 0:width, :] = (turned_ref[b].astype(F32) * weight.astype(F32)).astype(BF16)
        right_ref[b, width:, :] = jnp.broadcast_to(weight, (LANES, BLOCK))
    peers, own_tall, _ = out_ref.shape
    own = vehicles // peers
    half = peers // 2
    eye = diagonal((own, LANES))
    line = lax.broadcasted_iota(jnp.int32, (own_tall - own, LANES), 0)
    for k in range(vehicles // TALL):
        rows = pl.ds(k * TALL, TALL)
        num = sum(
            lax.dot_general(
                e_ref[b, rows, :], right_ref[b], LAST_DIMS, preferred_element_type=F32
            )
            for b in range(blocks)
        )
        for q in range(TALL // own):
            r = k * (TALL // own) + q
            to = (r % half) * 2 + r // half
            mine = num[q * own : (q + 1) * own]
            out_ref[to, 0:own, :] = mine[:, 0:width].astype(BF16)
            den = jnp.sum(jnp.where(eye, mine[:, width:], 0.0), axis=0, keepdims=True)
            high = den.astype(BF16).astype(F32)
            tail = jnp.where(line == 0, high, jnp.where(line == 1, den - high, 0.0))
            out_ref[to, own:own_tall, :] = tail.astype(BF16)


def second_pass(parts, turned, ints, e, peers):
    blocks, vehicles, _ = e.shape
    width = turned.shape[1]
    return pl.pallas_call(
        second_kernel,
        in_specs=[VMEM, VMEM, VMEM, VMEM],
        out_specs=VMEM,
        out_shape=jax.ShapeDtypeStruct((peers, vehicles // peers + 8, width), BF16),
        scratch_shapes=[
            pltpu.VMEM((vehicles, LANES), BF16),
            pltpu.VMEM((blocks, width + LANES, BLOCK), BF16),
        ],
        compiler_params=pltpu.CompilerParams(vmem_limit_bytes=SECOND_LIMIT),
        name="second_pass",
    )(parts, turned, ints, e)


def update_kernel(
    chips, part_ref, veh_ref, average_ref, identity_ref, offset_ref, projector_ref, out_ref
):
    own = part_ref.shape[1] - 8
    total = jnp.sum(part_ref[...].astype(F32), axis=0)
    den = total[own : own + 1, :] + total[own + 1 : own + 2, :]
    shape = (own, LANES)
    spread = jnp.where(diagonal(shape), jnp.broadcast_to(den, shape), 0.0)
    den = jnp.sum(spread, axis=1, keepdims=True)
    centroid = (total[0:own] / den).astype(BF16)
    y, x, pair, core = (lax.axis_index(name) for name in ("y", "x", "pair", "veh"))
    x_n, pair_n = lax.axis_size("x"), lax.axis_size("pair")
    where = core * chips + (y * x_n + x) * pair_n + pair
    rows = veh_ref[pl.ds(pl.multiple_of(where * own, own), own), :]
    pre = jnp.dot(centroid, average_ref[...], preferred_element_type=F32)
    pre = pre + jnp.dot(rows, identity_ref[...], preferred_element_type=F32) + offset_ref[...]
    hidden = jax.nn.silu(pre).astype(BF16)
    update = jnp.dot(hidden, projector_ref[...], preferred_element_type=F32)
    new = (rows.astype(F32) + update).astype(BF16)
    for r in range(out_ref.shape[0] // own):
        out_ref[pl.ds(r * own, own), :] = new


def update_rows(parts, veh, average, identity, offset, projector, copies):
    own = parts.shape[1] - 8
    return pl.pallas_call(
        functools.partial(update_kernel, copies),
        in_specs=[VMEM] * 6,
        out_specs=VMEM,
        out_shape=jax.ShapeDtypeStruct((copies * own, veh.shape[1]), BF16),
        compiler_params=pltpu.CompilerParams(vmem_limit_bytes=SMALL_LIMIT),
        name="update_rows",
    )(parts, veh, average, identity, offset, projector)


def swap(array, axes):
    return lax.all_to_all(array, axes, 0, 0, tiled=True)


def solution(mesh):
    stops_n = mesh.shape["stops"]
    y = x = 4
    pair = 2
    far = stops_n // (y * x * pair)
    inner = Mesh(
        mesh.devices.reshape(y, x, far, pair, mesh.shape["veh"]), ("y", "x", "far", "pair", "veh")
    )

    def on_device(
        customer_features,
        customer_loads,
        truck_limits,
        truck_features,
        customer_average_matrix,
        truck_identity_matrix,
        hidden_offset,
        output_projector,
    ):
        core = lax.axis_index("veh")
        half = core.astype(jnp.int32).reshape(1)
        chips = y * x * pair
        loads = customer_loads.reshape(-1, LANES)
        caps = truck_limits.reshape(-1, LANES)

        e, col, turned, ints = first_pass(
            half, truck_features, customer_features, loads, caps, far * pair
        )
        col = swap(col, ("far", "pair"))
        col = swap(sum_and_copy(col, y * x * 2), ("y", "x", "veh"))
        parts = second_pass(col, turned, ints, e, chips * 2)
        parts = swap(parts, ("y", "x", "pair", "veh"))
        parts = swap(sum_and_copy(parts, far), "far")
        new = update_rows(
            parts,
            truck_features,
            customer_average_matrix,
            truck_identity_matrix,
            hidden_offset.reshape(1, -1),
            output_projector,
            chips,
        )
        return swap(new, ("y", "x", "pair"))

    split = ("y", "x", "far", "pair")
    placed = (P(split, None), P(split), P(), P(), P(), P(), P(), P())
    return jax.shard_map(
        on_device, mesh=inner, in_specs=placed, out_specs=P("veh", None), check_vma=False
    )
```

```python
import functools

import jax
import jax.numpy as jnp
from jax import lax
from jax.experimental import pallas as pl
from jax.experimental.pallas import tpu as pltpu
from jax.sharding import Mesh, PartitionSpec as P

F32 = jnp.float32
BF16 = jnp.bfloat16
LANES = 128
BLOCK = 256
CHUNK = 256
TALL = 512
LOG2E = 1.4426950408889634
ROW_BITS = 90.0
CAP_SCALE = 2.0**-20
WEIGHT_SCALE = 2.0**50
FIRST_LIMIT = 48 << 20
SECOND_LIMIT = 16 << 20
SMALL_LIMIT = 4 << 20
LAST_DIMS = (((1,), (1,)), ((), ()))
VMEM = pl.BlockSpec(memory_space=pltpu.VMEM)
SMEM = pl.BlockSpec(memory_space=pltpu.SMEM)
ANY = pl.BlockSpec(memory_space=pl.ANY)


def diagonal(shape):
    n = len(shape)
    return lax.broadcasted_iota(jnp.int32, shape, n - 2) == lax.broadcasted_iota(
        jnp.int32, shape, n - 1
    )


def loads_of(ref, b):
    n = BLOCK // LANES
    return jnp.concatenate([ref[pl.ds(b * n + i, 1), :] for i in range(n)], axis=1).astype(F32)


def first_kernel(
    half_ref,
    veh_hbm,
    stop_hbm,
    load_hbm,
    cap_hbm,
    e_ref,
    out_ref,
    turned_ref,
    int_ref,
    veh_ref,
    stop_ref,
    z0_ref,
    z1_ref,
    share_ref,
    sem,
):
    vehicles, width = veh_ref.shape
    scale = LOG2E / width**0.5
    blocks = e_ref.shape[0]
    chunks = vehicles // CHUNK
    own = blocks * BLOCK
    tall = own // LANES
    half = half_ref[0]
    z_refs = (z0_ref, z1_ref)
    mine = pl.ds(pl.multiple_of(half * own, own), own)
    lines = pl.ds(pl.multiple_of(half * tall, tall), tall)
    moves = [
        pltpu.make_async_copy(veh_hbm, veh_ref, sem.at[0]),
        pltpu.make_async_copy(stop_hbm.at[mine], stop_ref, sem.at[1]),
        pltpu.make_async_copy(load_hbm.at[lines], int_ref.at[pl.ds(0, tall)], sem.at[2]),
        pltpu.make_async_copy(cap_hbm, int_ref.at[pl.ds(tall, cap_hbm.shape[0])], sem.at[3]),
    ]
    for i in (1, 0, 2, 3):
        moves[i].start()
    moves[1].wait()
    for b in range(blocks):
        turned_ref[b] = stop_ref[pl.ds(b * BLOCK, BLOCK), :].T
    for move in (moves[0], *moves[2:]):
        move.wait()
    lowest = jnp.full((8, BLOCK), -jnp.inf, F32)

    def turn(b):
        return turned_ref[b]

    def scores(z_ref, turned, c, top):
        rows = pl.ds(c * CHUNK, CHUNK)
        z = jnp.dot(veh_ref[rows, :], turned, preferred_element_type=F32)
        z = z * scale
        z_ref[rows, :] = z
        return jnp.maximum(top, jnp.max(z.reshape(CHUNK // 8, 8, BLOCK), axis=0))

    def exponentials(b, z_ref, top, c, total):
        rows = pl.ds(c * CHUNK, CHUNK)
        e = jnp.exp2(z_ref[rows, :] - top)
        e_ref[b, rows, :] = e.astype(BF16)
        return total + jnp.sum(e.reshape(CHUNK // 8, 8, BLOCK), axis=0)

    def level(top):
        return jnp.max(top, axis=0, keepdims=True) - ROW_BITS

    def step(b, slot, top, more):
        turned = turn(b + 1) if more else None
        after = lowest
        total = jnp.zeros((8, BLOCK), F32)
        for c in range(chunks):
            if more:
                after = scores(z_refs[1 - slot], turned, c, after)
            total = exponentials(b, z_refs[slot], top, c, total)
        total = jnp.sum(total, axis=0, keepdims=True)
        share = (loads_of(int_ref, b) / total).astype(BF16)
        share_ref[b] = jnp.broadcast_to(share, (LANES, BLOCK))
        return level(after)

    turned = turn(0)
    top = lowest
    for c in range(chunks):
        top = scores(z_refs[0], turned, c, top)
    top = level(top)

    def two(p, top):
        return step(2 * p + 1, 1, step(2 * p, 0, top, True), True)

    top = lax.fori_loop(0, blocks // 2 - 1, two, top)
    top = step(blocks - 2, 0, top, True)
    step(blocks - 1, 1, top, False)

    for k in range(vehicles // LANES):
        rows = pl.ds(k * LANES, LANES)
        col = jnp.zeros((LANES, LANES), F32)
        for b in range(blocks):
            t = e_ref[b, rows, :] * share_ref[b]
            t = t[:, 0:LANES] + t[:, LANES:BLOCK]
            col = col + t.astype(F32)
        col = jnp.sum(col.T, axis=0, keepdims=True).astype(out_ref.dtype)
        out_ref[:, k : k + 1, :] = jnp.broadcast_to(col[None], (out_ref.shape[0], 1, LANES))


def first_pass(half, veh, stops, loads, caps, peers):
    vehicles, width = veh.shape
    blocks = stops.shape[0] // 2 // BLOCK
    return pl.pallas_call(
        first_kernel,
        in_specs=[SMEM, ANY, ANY, ANY, ANY],
        out_specs=[VMEM, VMEM, VMEM, VMEM],
        out_shape=[
            pltpu.VMEM((blocks, vehicles, BLOCK), BF16),
            pltpu.VMEM((peers, vehicles // LANES, LANES), BF16),
            pltpu.VMEM((blocks, width, BLOCK), BF16),
            pltpu.VMEM((loads.shape[0] // 2 + caps.shape[0], LANES), jnp.int32),
        ],
        scratch_shapes=[
            pltpu.VMEM((vehicles, width), BF16),
            pltpu.VMEM((blocks * BLOCK, width), BF16),
            pltpu.VMEM((vehicles, BLOCK), F32),
            pltpu.VMEM((vehicles, BLOCK), F32),
            pltpu.VMEM((blocks, LANES, BLOCK), BF16),
            pltpu.SemaphoreType.DMA((4,)),
        ],
        compiler_params=pltpu.CompilerParams(vmem_limit_bytes=FIRST_LIMIT),
        name="first_pass",
    )(half, veh, stops, loads, caps)


def sum_and_copy_kernel(in_ref, out_ref):
    total = jnp.sum(in_ref[...].astype(F32), axis=0)
    out_ref[...] = jnp.broadcast_to(total.astype(out_ref.dtype)[None], out_ref.shape)


def sum_and_copy(parts, copies):
    return pl.pallas_call(
        sum_and_copy_kernel,
        in_specs=[VMEM],
        out_specs=VMEM,
        out_shape=jax.ShapeDtypeStruct((copies,) + parts.shape[1:], parts.dtype),
        compiler_params=pltpu.CompilerParams(vmem_limit_bytes=SMALL_LIMIT),
        name="sum_and_copy",
    )(parts)


def second_kernel(part_ref, turned_ref, int_ref, e_ref, own_ref, other_ref, g_ref, right_ref):
    blocks, vehicles, _ = e_ref.shape
    width = turned_ref.shape[1]
    lines = vehicles // LANES
    tall = int_ref.shape[0] - lines
    colsum = jnp.sum(part_ref[...].astype(F32), axis=0)
    g = (int_ref[tall:, :].astype(F32) * CAP_SCALE) / colsum
    square = (LANES, LANES)
    eye = diagonal(square)
    for r in range(lines):
        spread = jnp.where(eye, jnp.broadcast_to(g[r : r + 1], square), 0.0)
        column = jnp.sum(spread, axis=1, keepdims=True)
        g_ref[pl.ds(r * LANES, LANES), :] = jnp.broadcast_to(column, square).astype(BF16)

    for b in range(blocks):
        total = jnp.zeros((16, BLOCK), F32)
        for c in range(vehicles // CHUNK):
            rows = pl.ds(c * CHUNK, CHUNK)
            g = jnp.concatenate([g_ref[rows, :]] * (BLOCK // LANES), axis=1)
            t = (e_ref[b, rows, :] * g).reshape(CHUNK // 32, 2, 16, BLOCK)
            t = (t[:, 0] + t[:, 1]).astype(F32)
            total = total + jnp.sum(t, axis=0)
        total = jnp.sum(total, axis=0, keepdims=True)
        weight = (loads_of(int_ref, b) * WEIGHT_SCALE / total).astype(BF16)
        right_ref[b, 0:width, :] = (turned_ref[b].astype(F32) * weight.astype(F32)).astype(BF16)
        right_ref[b, width:, :] = jnp.broadcast_to(weight, (LANES, BLOCK))
    peers, own_tall, _ = own_ref.shape
    half = vehicles // 2
    own = half // peers
    eye = diagonal((own, LANES))
    line = lax.broadcasted_iota(jnp.int32, (own_tall - own, LANES), 0)
    core = lax.axis_index("veh")
    for out_ref, first in ((other_ref, (1 - core) * half), (own_ref, core * half)):
        for k in range(half // TALL):
            rows = pl.ds(pl.multiple_of(first + k * TALL, TALL), TALL)
            num = sum(
                lax.dot_general(
                    e_ref[b, rows, :], right_ref[b], LAST_DIMS, preferred_element_type=F32
                )
                for b in range(blocks)
            )
            for q in range(TALL // own):
                to = k * (TALL // own) + q
                mine = num[q * own : (q + 1) * own]
                out_ref[to, 0:own, :] = mine[:, 0:width].astype(out_ref.dtype)
                den = jnp.sum(jnp.where(eye, mine[:, width:], 0.0), axis=0, keepdims=True)
                high = den.astype(BF16).astype(F32)
                tail = jnp.where(line == 0, high, jnp.where(line == 1, den - high, 0.0))
                out_ref[to, own:own_tall, :] = tail.astype(out_ref.dtype)


def second_pass(parts, turned, ints, e, peers):
    blocks, vehicles, _ = e.shape
    width = turned.shape[1]
    return pl.pallas_call(
        second_kernel,
        in_specs=[VMEM, VMEM, VMEM, VMEM],
        out_specs=[VMEM, VMEM],
        out_shape=[
            jax.ShapeDtypeStruct((peers, vehicles // (2 * peers) + 8, width), F32),
            jax.ShapeDtypeStruct((peers, vehicles // (2 * peers) + 8, width), BF16),
        ],
        scratch_shapes=[
            pltpu.VMEM((vehicles, LANES), BF16),
            pltpu.VMEM((blocks, width + LANES, BLOCK), BF16),
        ],
        compiler_params=pltpu.CompilerParams(vmem_limit_bytes=SECOND_LIMIT),
        name="second_pass",
    )(parts, turned, ints, e)


def join_kernel(own_ref, sent_ref, out_ref):
    own = own_ref[...]
    tall = own.shape[1]
    total = own + sent_ref[1 - lax.axis_index("veh")].astype(F32)
    den = total[:, tall - 8 : tall - 7] + total[:, tall - 7 : tall - 6]
    high = den.astype(BF16).astype(F32)
    line = lax.broadcasted_iota(jnp.int32, (1, 8, LANES), 1)
    tail = jnp.where(line == 0, high, jnp.where(line == 1, den - high, 0.0))
    out_ref[:, : tall - 8, :] = total[:, : tall - 8].astype(BF16)
    out_ref[:, tall - 8 :, :] = tail.astype(BF16)


def join_cores(own, sent):
    return pl.pallas_call(
        join_kernel,
        in_specs=[VMEM, VMEM],
        out_specs=VMEM,
        out_shape=jax.ShapeDtypeStruct(own.shape, BF16),
        compiler_params=pltpu.CompilerParams(vmem_limit_bytes=SMALL_LIMIT),
        name="join_cores",
    )(own, sent)


def update_kernel(
    chips, part_ref, veh_ref, average_ref, identity_ref, offset_ref, projector_ref, out_ref
):
    own = part_ref.shape[1] - 8
    total = jnp.sum(part_ref[...].astype(F32), axis=0)
    den = total[own : own + 1, :] + total[own + 1 : own + 2, :]
    shape = (own, LANES)
    spread = jnp.where(diagonal(shape), jnp.broadcast_to(den, shape), 0.0)
    den = jnp.sum(spread, axis=1, keepdims=True)
    centroid = (total[0:own] / den).astype(BF16)
    y, x, pair, core = (lax.axis_index(name) for name in ("y", "x", "pair", "veh"))
    x_n, pair_n = lax.axis_size("x"), lax.axis_size("pair")
    where = core * chips + (y * x_n + x) * pair_n + pair
    rows = veh_ref[pl.ds(pl.multiple_of(where * own, own), own), :]
    pre = jnp.dot(centroid, average_ref[...], preferred_element_type=F32)
    pre = pre + jnp.dot(rows, identity_ref[...], preferred_element_type=F32) + offset_ref[...]
    hidden = jax.nn.silu(pre).astype(BF16)
    update = jnp.dot(hidden, projector_ref[...], preferred_element_type=F32)
    new = (rows.astype(F32) + update).astype(BF16)
    for r in range(out_ref.shape[0] // own):
        out_ref[pl.ds(r * own, own), :] = new


def update_rows(parts, veh, average, identity, offset, projector, copies):
    own = parts.shape[1] - 8
    return pl.pallas_call(
        functools.partial(update_kernel, copies),
        in_specs=[VMEM] * 6,
        out_specs=VMEM,
        out_shape=jax.ShapeDtypeStruct((copies * own, veh.shape[1]), BF16),
        compiler_params=pltpu.CompilerParams(vmem_limit_bytes=SMALL_LIMIT),
        name="update_rows",
    )(parts, veh, average, identity, offset, projector)


def swap(array, axes):
    return lax.all_to_all(array, axes, 0, 0, tiled=True)


def solution(mesh):
    stops_n = mesh.shape["stops"]
    y = x = 4
    pair = 2
    far = stops_n // (y * x * pair)
    inner = Mesh(
        mesh.devices.reshape(y, x, far, pair, mesh.shape["veh"]), ("y", "x", "far", "pair", "veh")
    )

    def on_device(
        customer_features,
        customer_loads,
        truck_limits,
        truck_features,
        customer_average_matrix,
        truck_identity_matrix,
        hidden_offset,
        output_projector,
    ):
        core = lax.axis_index("veh")
        half = core.astype(jnp.int32).reshape(1)
        chips = y * x * pair
        loads = customer_loads.reshape(-1, LANES)
        caps = truck_limits.reshape(-1, LANES)

        e, col, turned, ints = first_pass(
            half, truck_features, customer_features, loads, caps, far * pair
        )
        col = swap(col, ("far", "pair"))
        col = swap(sum_and_copy(col, y * x * 2), ("y", "x", "veh"))
        own, other = second_pass(col, turned, ints, e, chips)
        parts = join_cores(own, lax.all_gather(other, "veh"))
        parts = swap(parts, ("y", "x", "pair"))
        parts = swap(sum_and_copy(parts, far), "far")
        new = update_rows(
            parts,
            truck_features,
            customer_average_matrix,
            truck_identity_matrix,
            hidden_offset.reshape(1, -1),
            output_projector,
            chips,
        )
        return swap(new, ("y", "x", "pair"))

    split = ("y", "x", "far", "pair")
    placed = (P(split, None), P(split), P(), P(), P(), P(), P(), P())
    return jax.shard_map(
        on_device, mesh=inner, in_specs=placed, out_specs=P("veh", None), check_vma=False
    )
```

```python
import functools

import jax
import jax.numpy as jnp
from jax import lax
from jax.experimental import pallas as pl
from jax.experimental.pallas import tpu as pltpu
from jax.sharding import Mesh, PartitionSpec as P

F32 = jnp.float32
BF16 = jnp.bfloat16
LANES = 128
BLOCK = 256
CHUNK = 512
TALL = 512
LOG2E = 1.4426950408889634
ROW_BITS = 90.0
CAP_SCALE = 2.0**-20
WEIGHT_SCALE = 2.0**50
FIRST_LIMIT = 48 << 20
SECOND_LIMIT = 16 << 20
SMALL_LIMIT = 4 << 20
LAST_DIMS = (((1,), (1,)), ((), ()))
VMEM = pl.BlockSpec(memory_space=pltpu.VMEM)
SMEM = pl.BlockSpec(memory_space=pltpu.SMEM)
ANY = pl.BlockSpec(memory_space=pl.ANY)


def diagonal(shape):
    n = len(shape)
    return lax.broadcasted_iota(jnp.int32, shape, n - 2) == lax.broadcasted_iota(
        jnp.int32, shape, n - 1
    )


def loads_of(ref, b):
    n = BLOCK // LANES
    return jnp.concatenate([ref[pl.ds(b * n + i, 1), :] for i in range(n)], axis=1).astype(F32)


def first_kernel(
    half_ref,
    veh_hbm,
    stop_hbm,
    load_hbm,
    cap_hbm,
    e_ref,
    out_ref,
    turned_ref,
    int_ref,
    veh_ref,
    stop_ref,
    z0_ref,
    z1_ref,
    share_ref,
    sem,
):
    vehicles, width = veh_ref.shape
    scale = LOG2E / width**0.5
    blocks = e_ref.shape[0]
    chunks = vehicles // CHUNK
    own = blocks * BLOCK
    tall = own // LANES
    half = half_ref[0]
    z_refs = (z0_ref, z1_ref)
    mine = pl.ds(pl.multiple_of(half * own, own), own)
    lines = pl.ds(pl.multiple_of(half * tall, tall), tall)
    moves = [
        pltpu.make_async_copy(veh_hbm, veh_ref, sem.at[0]),
        pltpu.make_async_copy(stop_hbm.at[mine], stop_ref, sem.at[1]),
        pltpu.make_async_copy(load_hbm.at[lines], int_ref.at[pl.ds(0, tall)], sem.at[2]),
        pltpu.make_async_copy(cap_hbm, int_ref.at[pl.ds(tall, cap_hbm.shape[0])], sem.at[3]),
    ]
    for i in (1, 0, 2, 3):
        moves[i].start()
    moves[1].wait()
    for b in range(blocks):
        turned_ref[b] = stop_ref[pl.ds(b * BLOCK, BLOCK), :].T
    for move in (moves[0], *moves[2:]):
        move.wait()
    lowest = jnp.full((8, BLOCK), -jnp.inf, F32)

    def turn(b):
        return turned_ref[b]

    def scores(z_ref, turned, c, top):
        rows = pl.ds(c * CHUNK, CHUNK)
        z = jnp.dot(veh_ref[rows, :], turned, preferred_element_type=F32)
        z = z * scale
        z_ref[rows, :] = z
        return jnp.maximum(top, jnp.max(z.reshape(CHUNK // 8, 8, BLOCK), axis=0))

    def exponentials(b, z_ref, top, c, total):
        rows = pl.ds(c * CHUNK, CHUNK)
        e = jnp.exp2(z_ref[rows, :] - top)
        e_ref[b, rows, :] = e.astype(BF16)
        return total + jnp.sum(e.reshape(CHUNK // 8, 8, BLOCK), axis=0)

    def level(top):
        return jnp.max(top, axis=0, keepdims=True) - ROW_BITS

    def step(b, slot, top, more):
        turned = turn(b + 1) if more else None
        after = lowest
        total = jnp.zeros((8, BLOCK), F32)
        for c in range(chunks):
            if more:
                after = scores(z_refs[1 - slot], turned, c, after)
            total = exponentials(b, z_refs[slot], top, c, total)
        total = jnp.sum(total, axis=0, keepdims=True)
        share = (loads_of(int_ref, b) / total).astype(BF16)
        share_ref[b] = jnp.broadcast_to(share, (LANES, BLOCK))
        return level(after)

    turned = turn(0)
    top = lowest
    for c in range(chunks):
        top = scores(z_refs[0], turned, c, top)
    top = level(top)

    def two(p, top):
        return step(2 * p + 1, 1, step(2 * p, 0, top, True), True)

    top = lax.fori_loop(0, blocks // 2 - 1, two, top)
    top = step(blocks - 2, 0, top, True)
    step(blocks - 1, 1, top, False)

    for k in range(vehicles // LANES):
        rows = pl.ds(k * LANES, LANES)
        col = jnp.zeros((LANES, LANES), F32)
        for b in range(0, blocks, 2):
            t = e_ref[b, rows, :] * share_ref[b] + e_ref[b + 1, rows, :] * share_ref[b + 1]
            t = t[:, 0:LANES] + t[:, LANES:BLOCK]
            col = col + t.astype(F32)
        col = jnp.sum(col.T, axis=0, keepdims=True).astype(out_ref.dtype)
        out_ref[:, k : k + 1, :] = jnp.broadcast_to(col[None], (out_ref.shape[0], 1, LANES))


def first_pass(half, veh, stops, loads, caps, peers):
    vehicles, width = veh.shape
    blocks = stops.shape[0] // 2 // BLOCK
    return pl.pallas_call(
        first_kernel,
        in_specs=[SMEM, ANY, ANY, ANY, ANY],
        out_specs=[VMEM, VMEM, VMEM, VMEM],
        out_shape=[
            pltpu.VMEM((blocks, vehicles, BLOCK), BF16),
            pltpu.VMEM((peers, vehicles // LANES, LANES), BF16),
            pltpu.VMEM((blocks, width, BLOCK), BF16),
            pltpu.VMEM((loads.shape[0] // 2 + caps.shape[0], LANES), jnp.int32),
        ],
        scratch_shapes=[
            pltpu.VMEM((vehicles, width), BF16),
            pltpu.VMEM((blocks * BLOCK, width), BF16),
            pltpu.VMEM((vehicles, BLOCK), F32),
            pltpu.VMEM((vehicles, BLOCK), F32),
            pltpu.VMEM((blocks, LANES, BLOCK), BF16),
            pltpu.SemaphoreType.DMA((4,)),
        ],
        compiler_params=pltpu.CompilerParams(vmem_limit_bytes=FIRST_LIMIT),
        name="first_pass",
    )(half, veh, stops, loads, caps)


def sum_and_copy_kernel(in_ref, out_ref):
    total = jnp.sum(in_ref[...].astype(F32), axis=0)
    out_ref[...] = jnp.broadcast_to(total.astype(out_ref.dtype)[None], out_ref.shape)


def sum_and_copy(parts, copies):
    return pl.pallas_call(
        sum_and_copy_kernel,
        in_specs=[VMEM],
        out_specs=VMEM,
        out_shape=jax.ShapeDtypeStruct((copies,) + parts.shape[1:], parts.dtype),
        compiler_params=pltpu.CompilerParams(vmem_limit_bytes=SMALL_LIMIT),
        name="sum_and_copy",
    )(parts)


def second_kernel(part_ref, turned_ref, int_ref, e_ref, own_ref, other_ref, g_ref, right_ref):
    blocks, vehicles, _ = e_ref.shape
    width = turned_ref.shape[1]
    lines = vehicles // LANES
    tall = int_ref.shape[0] - lines
    colsum = jnp.sum(part_ref[...].astype(F32), axis=0)
    g = (int_ref[tall:, :].astype(F32) * CAP_SCALE) / colsum
    square = (LANES, LANES)
    eye = diagonal(square)
    for r in range(lines):
        spread = jnp.where(eye, jnp.broadcast_to(g[r : r + 1], square), 0.0)
        column = jnp.sum(spread, axis=1, keepdims=True)
        g_ref[pl.ds(r * LANES, LANES), :] = jnp.broadcast_to(column, square).astype(BF16)

    for b in range(blocks):
        total = jnp.zeros((16, BLOCK), F32)
        for c in range(vehicles // CHUNK):
            rows = pl.ds(c * CHUNK, CHUNK)
            g = jnp.concatenate([g_ref[rows, :]] * (BLOCK // LANES), axis=1)
            t = (e_ref[b, rows, :] * g).reshape(CHUNK // 64, 4, 16, BLOCK)
            t = ((t[:, 0] + t[:, 1]) + (t[:, 2] + t[:, 3])).astype(F32)
            total = total + jnp.sum(t, axis=0)
        total = jnp.sum(total, axis=0, keepdims=True)
        weight = (loads_of(int_ref, b) * WEIGHT_SCALE / total).astype(BF16)
        right_ref[b, 0:width, :] = (turned_ref[b].astype(F32) * weight.astype(F32)).astype(BF16)
        right_ref[b, width:, :] = jnp.broadcast_to(weight, (LANES, BLOCK))
    peers, own_tall, _ = own_ref.shape
    half = vehicles // 2
    own = half // peers
    eye = diagonal((own, LANES))
    line = lax.broadcasted_iota(jnp.int32, (own_tall - own, LANES), 0)
    core = lax.axis_index("veh")
    for out_ref, first in ((other_ref, (1 - core) * half), (own_ref, core * half)):
        for k in range(half // TALL):
            rows = pl.ds(pl.multiple_of(first + k * TALL, TALL), TALL)
            num = sum(
                lax.dot_general(
                    e_ref[b, rows, :], right_ref[b], LAST_DIMS, preferred_element_type=F32
                )
                for b in range(blocks)
            )
            for q in range(TALL // own):
                to = k * (TALL // own) + q
                mine = num[q * own : (q + 1) * own]
                out_ref[to, 0:own, :] = mine[:, 0:width].astype(out_ref.dtype)
                den = jnp.sum(jnp.where(eye, mine[:, width:], 0.0), axis=0, keepdims=True)
                high = den.astype(BF16).astype(F32)
                tail = jnp.where(line == 0, high, jnp.where(line == 1, den - high, 0.0))
                out_ref[to, own:own_tall, :] = tail.astype(out_ref.dtype)


def second_pass(parts, turned, ints, e, peers):
    blocks, vehicles, _ = e.shape
    width = turned.shape[1]
    return pl.pallas_call(
        second_kernel,
        in_specs=[VMEM, VMEM, VMEM, VMEM],
        out_specs=[VMEM, VMEM],
        out_shape=[
            jax.ShapeDtypeStruct((peers, vehicles // (2 * peers) + 8, width), F32),
            jax.ShapeDtypeStruct((peers, vehicles // (2 * peers) + 8, width), BF16),
        ],
        scratch_shapes=[
            pltpu.VMEM((vehicles, LANES), BF16),
            pltpu.VMEM((blocks, width + LANES, BLOCK), BF16),
        ],
        compiler_params=pltpu.CompilerParams(vmem_limit_bytes=SECOND_LIMIT),
        name="second_pass",
    )(parts, turned, ints, e)


def join_kernel(own_ref, sent_ref, out_ref):
    own = own_ref[...]
    tall = own.shape[1]
    total = own + sent_ref[1 - lax.axis_index("veh")].astype(F32)
    den = total[:, tall - 8 : tall - 7] + total[:, tall - 7 : tall - 6]
    high = den.astype(BF16).astype(F32)
    line = lax.broadcasted_iota(jnp.int32, (1, 8, LANES), 1)
    tail = jnp.where(line == 0, high, jnp.where(line == 1, den - high, 0.0))
    out_ref[:, : tall - 8, :] = total[:, : tall - 8].astype(BF16)
    out_ref[:, tall - 8 :, :] = tail.astype(BF16)


def join_cores(own, sent):
    return pl.pallas_call(
        join_kernel,
        in_specs=[VMEM, VMEM],
        out_specs=VMEM,
        out_shape=jax.ShapeDtypeStruct(own.shape, BF16),
        compiler_params=pltpu.CompilerParams(vmem_limit_bytes=SMALL_LIMIT),
        name="join_cores",
    )(own, sent)


def update_kernel(
    chips, part_ref, veh_ref, average_ref, identity_ref, offset_ref, projector_ref, out_ref
):
    own = part_ref.shape[1] - 8
    total = jnp.sum(part_ref[...].astype(F32), axis=0)
    den = total[own : own + 1, :] + total[own + 1 : own + 2, :]
    shape = (own, LANES)
    spread = jnp.where(diagonal(shape), jnp.broadcast_to(den, shape), 0.0)
    den = jnp.sum(spread, axis=1, keepdims=True)
    centroid = (total[0:own] / den).astype(BF16)
    y, x, pair, core = (lax.axis_index(name) for name in ("y", "x", "pair", "veh"))
    x_n, pair_n = lax.axis_size("x"), lax.axis_size("pair")
    where = core * chips + (y * x_n + x) * pair_n + pair
    rows = veh_ref[pl.ds(pl.multiple_of(where * own, own), own), :]
    pre = jnp.dot(centroid, average_ref[...], preferred_element_type=F32)
    pre = pre + jnp.dot(rows, identity_ref[...], preferred_element_type=F32) + offset_ref[...]
    hidden = jax.nn.silu(pre).astype(BF16)
    update = jnp.dot(hidden, projector_ref[...], preferred_element_type=F32)
    new = (rows.astype(F32) + update).astype(BF16)
    for r in range(out_ref.shape[0] // own):
        out_ref[pl.ds(r * own, own), :] = new


def update_rows(parts, veh, average, identity, offset, projector, copies):
    own = parts.shape[1] - 8
    return pl.pallas_call(
        functools.partial(update_kernel, copies),
        in_specs=[VMEM] * 6,
        out_specs=VMEM,
        out_shape=jax.ShapeDtypeStruct((copies * own, veh.shape[1]), BF16),
        compiler_params=pltpu.CompilerParams(vmem_limit_bytes=SMALL_LIMIT),
        name="update_rows",
    )(parts, veh, average, identity, offset, projector)


def swap(array, axes):
    return lax.all_to_all(array, axes, 0, 0, tiled=True)


def solution(mesh):
    stops_n = mesh.shape["stops"]
    y = x = 4
    pair = 2
    far = stops_n // (y * x * pair)
    inner = Mesh(
        mesh.devices.reshape(y, x, far, pair, mesh.shape["veh"]), ("y", "x", "far", "pair", "veh")
    )

    def on_device(
        customer_features,
        customer_loads,
        truck_limits,
        truck_features,
        customer_average_matrix,
        truck_identity_matrix,
        hidden_offset,
        output_projector,
    ):
        core = lax.axis_index("veh")
        half = core.astype(jnp.int32).reshape(1)
        chips = y * x * pair
        loads = customer_loads.reshape(-1, LANES)
        caps = truck_limits.reshape(-1, LANES)

        e, col, turned, ints = first_pass(
            half, truck_features, customer_features, loads, caps, far * pair
        )
        col = swap(col, ("far", "pair"))
        col = swap(sum_and_copy(col, y * x * 2), ("y", "x", "veh"))
        own, other = second_pass(col, turned, ints, e, chips)
        parts = join_cores(own, lax.all_gather(other, "veh"))
        parts = swap(parts, ("y", "x", "pair"))
        parts = swap(sum_and_copy(parts, far), "far")
        new = update_rows(
            parts,
            truck_features,
            customer_average_matrix,
            truck_identity_matrix,
            hidden_offset.reshape(1, -1),
            output_projector,
            chips,
        )
        return swap(new, ("y", "x", "pair"))

    split = ("y", "x", "far", "pair")
    placed = (P(split, None), P(split), P(), P(), P(), P(), P(), P())
    return jax.shard_map(
        on_device, mesh=inner, in_specs=placed, out_specs=P("veh", None), check_vma=False
    )
```

```python
import functools

import jax
import jax.numpy as jnp
from jax import lax
from jax.experimental import pallas as pl
from jax.experimental.pallas import tpu as pltpu
from jax.sharding import Mesh, PartitionSpec as P

F32 = jnp.float32
BF16 = jnp.bfloat16
LANES = 128
BLOCK = 256
CHUNK = 512
TALL = 512
LOG2E = 1.4426950408889634
ROW_BITS = 90.0
CAP_SCALE = 2.0**-20
WEIGHT_SCALE = 2.0**50
FIRST_LIMIT = 48 << 20
SECOND_LIMIT = 16 << 20
SMALL_LIMIT = 4 << 20
LAST_DIMS = (((1,), (1,)), ((), ()))
VMEM = pl.BlockSpec(memory_space=pltpu.VMEM)
SMEM = pl.BlockSpec(memory_space=pltpu.SMEM)
ANY = pl.BlockSpec(memory_space=pl.ANY)


def diagonal(shape):
    n = len(shape)
    return lax.broadcasted_iota(jnp.int32, shape, n - 2) == lax.broadcasted_iota(
        jnp.int32, shape, n - 1
    )


def loads_of(ref, b):
    n = BLOCK // LANES
    return jnp.concatenate([ref[pl.ds(b * n + i, 1), :] for i in range(n)], axis=1).astype(F32)


def first_kernel(
    half_ref,
    veh_hbm,
    stop_hbm,
    load_hbm,
    cap_hbm,
    e_ref,
    out_ref,
    turned_ref,
    int_ref,
    veh_ref,
    stop_ref,
    z0_ref,
    z1_ref,
    share_ref,
    sem,
):
    vehicles, width = veh_ref.shape
    scale = LOG2E / width**0.5
    blocks = e_ref.shape[0]
    chunks = vehicles // CHUNK
    own = blocks * BLOCK
    tall = own // LANES
    half = half_ref[0]
    z_refs = (z0_ref, z1_ref)
    mine = pl.ds(pl.multiple_of(half * own, own), own)
    lines = pl.ds(pl.multiple_of(half * tall, tall), tall)
    moves = [
        pltpu.make_async_copy(veh_hbm, veh_ref, sem.at[0]),
        pltpu.make_async_copy(stop_hbm.at[mine], stop_ref, sem.at[1]),
        pltpu.make_async_copy(load_hbm.at[lines], int_ref.at[pl.ds(0, tall)], sem.at[2]),
        pltpu.make_async_copy(cap_hbm, int_ref.at[pl.ds(tall, cap_hbm.shape[0])], sem.at[3]),
    ]
    for i in (1, 0, 2, 3):
        moves[i].start()
    moves[1].wait()
    for b in range(blocks):
        turned_ref[b] = stop_ref[pl.ds(b * BLOCK, BLOCK), :].T
    for move in (moves[0], *moves[2:]):
        move.wait()
    lowest = jnp.full((8, BLOCK), -jnp.inf, F32)

    def turn(b):
        return turned_ref[b]

    def scores(z_ref, turned, c, top):
        rows = pl.ds(c * CHUNK, CHUNK)
        z = jnp.dot(veh_ref[rows, :], turned, preferred_element_type=F32)
        z = z * scale
        z_ref[rows, :] = z
        return jnp.maximum(top, jnp.max(z.reshape(CHUNK // 8, 8, BLOCK), axis=0))

    def exponentials(b, z_ref, top, c, total):
        rows = pl.ds(c * CHUNK, CHUNK)
        e = jnp.exp2(z_ref[rows, :] - top)
        e_ref[b, rows, :] = e.astype(BF16)
        return total + jnp.sum(e.reshape(CHUNK // 8, 8, BLOCK), axis=0)

    def level(top):
        return jnp.max(top, axis=0, keepdims=True) - ROW_BITS

    def step(b, slot, top, more):
        turned = turn(b + 1) if more else None
        after = lowest
        total = jnp.zeros((8, BLOCK), F32)
        for c in range(chunks):
            if more:
                after = scores(z_refs[1 - slot], turned, c, after)
            total = exponentials(b, z_refs[slot], top, c, total)
        total = jnp.sum(total, axis=0, keepdims=True)
        share = (loads_of(int_ref, b) / total).astype(BF16)
        share_ref[b] = jnp.broadcast_to(share, (LANES, BLOCK))
        return level(after)

    turned = turn(0)
    top = lowest
    for c in range(chunks):
        top = scores(z_refs[0], turned, c, top)
    top = level(top)

    def two(p, top):
        return step(2 * p + 1, 1, step(2 * p, 0, top, True), True)

    top = lax.fori_loop(0, blocks // 2 - 1, two, top)
    top = step(blocks - 2, 0, top, True)
    step(blocks - 1, 1, top, False)

    for k in range(vehicles // LANES):
        rows = pl.ds(k * LANES, LANES)
        col = jnp.zeros((LANES, LANES), F32)
        for b in range(0, blocks, 2):
            t = e_ref[b, rows, :] * share_ref[b] + e_ref[b + 1, rows, :] * share_ref[b + 1]
            t = t[:, 0:LANES] + t[:, LANES:BLOCK]
            col = col + t.astype(F32)
        col = jnp.sum(col.T, axis=0, keepdims=True).astype(out_ref.dtype)
        out_ref[:, k : k + 1, :] = jnp.broadcast_to(col[None], (out_ref.shape[0], 1, LANES))


def first_pass(half, veh, stops, loads, caps, peers):
    vehicles, width = veh.shape
    blocks = stops.shape[0] // 2 // BLOCK
    return pl.pallas_call(
        first_kernel,
        in_specs=[SMEM, ANY, ANY, ANY, ANY],
        out_specs=[VMEM, VMEM, VMEM, VMEM],
        out_shape=[
            pltpu.VMEM((blocks, vehicles, BLOCK), BF16),
            pltpu.VMEM((peers, vehicles // LANES, LANES), BF16),
            pltpu.VMEM((blocks, width, BLOCK), BF16),
            pltpu.VMEM((loads.shape[0] // 2 + caps.shape[0], LANES), jnp.int32),
        ],
        scratch_shapes=[
            pltpu.VMEM((vehicles, width), BF16),
            pltpu.VMEM((blocks * BLOCK, width), BF16),
            pltpu.VMEM((vehicles, BLOCK), F32),
            pltpu.VMEM((vehicles, BLOCK), F32),
            pltpu.VMEM((blocks, LANES, BLOCK), BF16),
            pltpu.SemaphoreType.DMA((4,)),
        ],
        compiler_params=pltpu.CompilerParams(vmem_limit_bytes=FIRST_LIMIT),
        name="first_pass",
    )(half, veh, stops, loads, caps)


def sum_and_copy_kernel(in_ref, out_ref):
    total = jnp.sum(in_ref[...].astype(F32), axis=0)
    out_ref[...] = jnp.broadcast_to(total.astype(out_ref.dtype)[None], out_ref.shape)


def sum_and_copy(parts, copies):
    return pl.pallas_call(
        sum_and_copy_kernel,
        in_specs=[VMEM],
        out_specs=VMEM,
        out_shape=jax.ShapeDtypeStruct((copies,) + parts.shape[1:], parts.dtype),
        compiler_params=pltpu.CompilerParams(vmem_limit_bytes=SMALL_LIMIT),
        name="sum_and_copy",
    )(parts)


def second_kernel(part_ref, turned_ref, int_ref, e_ref, own_ref, other_ref, g_ref, right_ref):
    blocks, vehicles, _ = e_ref.shape
    width = turned_ref.shape[1]
    lines = vehicles // LANES
    tall = int_ref.shape[0] - lines
    colsum = jnp.sum(part_ref[...].astype(F32), axis=0)
    g = (int_ref[tall:, :].astype(F32) * CAP_SCALE) / colsum
    square = (LANES, LANES)
    eye = diagonal(square)
    for r in range(lines):
        spread = jnp.where(eye, jnp.broadcast_to(g[r : r + 1], square), 0.0)
        column = jnp.sum(spread, axis=1, keepdims=True)
        g_ref[pl.ds(r * LANES, LANES), :] = jnp.broadcast_to(column, square).astype(BF16)

    for b in range(blocks):
        total = jnp.zeros((16, BLOCK), F32)
        for c in range(vehicles // CHUNK):
            rows = pl.ds(c * CHUNK, CHUNK)
            g = jnp.concatenate([g_ref[rows, :]] * (BLOCK // LANES), axis=1)
            t = (e_ref[b, rows, :] * g).reshape(CHUNK // 128, 8, 16, BLOCK)
            t = [t[:, 2 * i] + t[:, 2 * i + 1] for i in range(4)]
            t = ((t[0] + t[1]) + (t[2] + t[3])).astype(F32)
            total = total + jnp.sum(t, axis=0)
        total = jnp.sum(total, axis=0, keepdims=True)
        weight = (loads_of(int_ref, b) * WEIGHT_SCALE / total).astype(BF16)
        right_ref[b, 0:width, :] = (turned_ref[b].astype(F32) * weight.astype(F32)).astype(BF16)
        right_ref[b, width:, :] = jnp.broadcast_to(weight, (LANES, BLOCK))
    peers, own_tall, _ = own_ref.shape
    half = vehicles // 2
    own = half // peers
    eye = diagonal((own, LANES))
    line = lax.broadcasted_iota(jnp.int32, (own_tall - own, LANES), 0)
    core = lax.axis_index("veh")
    for out_ref, first in ((other_ref, (1 - core) * half), (own_ref, core * half)):
        for k in range(half // TALL):
            rows = pl.ds(pl.multiple_of(first + k * TALL, TALL), TALL)
            num = sum(
                lax.dot_general(
                    e_ref[b, rows, :], right_ref[b], LAST_DIMS, preferred_element_type=F32
                )
                for b in range(blocks)
            )
            for q in range(TALL // own):
                to = k * (TALL // own) + q
                mine = num[q * own : (q + 1) * own]
                out_ref[to, 0:own, :] = mine[:, 0:width].astype(out_ref.dtype)
                den = jnp.sum(jnp.where(eye, mine[:, width:], 0.0), axis=0, keepdims=True)
                high = den.astype(BF16).astype(F32)
                tail = jnp.where(line == 0, high, jnp.where(line == 1, den - high, 0.0))
                out_ref[to, own:own_tall, :] = tail.astype(out_ref.dtype)


def second_pass(parts, turned, ints, e, peers):
    blocks, vehicles, _ = e.shape
    width = turned.shape[1]
    return pl.pallas_call(
        second_kernel,
        in_specs=[VMEM, VMEM, VMEM, VMEM],
        out_specs=[VMEM, VMEM],
        out_shape=[
            jax.ShapeDtypeStruct((peers, vehicles // (2 * peers) + 8, width), F32),
            jax.ShapeDtypeStruct((peers, vehicles // (2 * peers) + 8, width), BF16),
        ],
        scratch_shapes=[
            pltpu.VMEM((vehicles, LANES), BF16),
            pltpu.VMEM((blocks, width + LANES, BLOCK), BF16),
        ],
        compiler_params=pltpu.CompilerParams(vmem_limit_bytes=SECOND_LIMIT),
        name="second_pass",
    )(parts, turned, ints, e)


def join_kernel(own_ref, sent_ref, out_ref):
    own = own_ref[...]
    tall = own.shape[1]
    total = own + sent_ref[1 - lax.axis_index("veh")].astype(F32)
    den = total[:, tall - 8 : tall - 7] + total[:, tall - 7 : tall - 6]
    high = den.astype(BF16).astype(F32)
    line = lax.broadcasted_iota(jnp.int32, (1, 8, LANES), 1)
    tail = jnp.where(line == 0, high, jnp.where(line == 1, den - high, 0.0))
    out_ref[:, : tall - 8, :] = total[:, : tall - 8].astype(BF16)
    out_ref[:, tall - 8 :, :] = tail.astype(BF16)


def join_cores(own, sent):
    return pl.pallas_call(
        join_kernel,
        in_specs=[VMEM, VMEM],
        out_specs=VMEM,
        out_shape=jax.ShapeDtypeStruct(own.shape, BF16),
        compiler_params=pltpu.CompilerParams(vmem_limit_bytes=SMALL_LIMIT),
        name="join_cores",
    )(own, sent)


def update_kernel(
    chips, part_ref, veh_ref, average_ref, identity_ref, offset_ref, projector_ref, out_ref
):
    own = part_ref.shape[1] - 8
    total = jnp.sum(part_ref[...].astype(F32), axis=0)
    den = total[own : own + 1, :] + total[own + 1 : own + 2, :]
    shape = (own, LANES)
    spread = jnp.where(diagonal(shape), jnp.broadcast_to(den, shape), 0.0)
    den = jnp.sum(spread, axis=1, keepdims=True)
    centroid = (total[0:own] / den).astype(BF16)
    y, x, pair, core = (lax.axis_index(name) for name in ("y", "x", "pair", "veh"))
    x_n, pair_n = lax.axis_size("x"), lax.axis_size("pair")
    where = core * chips + (y * x_n + x) * pair_n + pair
    rows = veh_ref[pl.ds(pl.multiple_of(where * own, own), own), :]
    pre = jnp.dot(centroid, average_ref[...], preferred_element_type=F32)
    pre = pre + jnp.dot(rows, identity_ref[...], preferred_element_type=F32) + offset_ref[...]
    hidden = jax.nn.silu(pre).astype(BF16)
    update = jnp.dot(hidden, projector_ref[...], preferred_element_type=F32)
    new = (rows.astype(F32) + update).astype(BF16)
    for r in range(out_ref.shape[0] // own):
        out_ref[pl.ds(r * own, own), :] = new


def update_rows(parts, veh, average, identity, offset, projector, copies):
    own = parts.shape[1] - 8
    return pl.pallas_call(
        functools.partial(update_kernel, copies),
        in_specs=[VMEM] * 6,
        out_specs=VMEM,
        out_shape=jax.ShapeDtypeStruct((copies * own, veh.shape[1]), BF16),
        compiler_params=pltpu.CompilerParams(vmem_limit_bytes=SMALL_LIMIT),
        name="update_rows",
    )(parts, veh, average, identity, offset, projector)


def swap(array, axes):
    return lax.all_to_all(array, axes, 0, 0, tiled=True)


def solution(mesh):
    stops_n = mesh.shape["stops"]
    y = x = 4
    pair = 2
    far = stops_n // (y * x * pair)
    inner = Mesh(
        mesh.devices.reshape(y, x, far, pair, mesh.shape["veh"]), ("y", "x", "far", "pair", "veh")
    )

    def on_device(
        customer_features,
        customer_loads,
        truck_limits,
        truck_features,
        customer_average_matrix,
        truck_identity_matrix,
        hidden_offset,
        output_projector,
    ):
        core = lax.axis_index("veh")
        half = core.astype(jnp.int32).reshape(1)
        chips = y * x * pair
        loads = customer_loads.reshape(-1, LANES)
        caps = truck_limits.reshape(-1, LANES)

        e, col, turned, ints = first_pass(
            half, truck_features, customer_features, loads, caps, far * pair
        )
        col = swap(col, ("far", "pair"))
        col = swap(sum_and_copy(col, y * x * 2), ("y", "x", "veh"))
        own, other = second_pass(col, turned, ints, e, chips)
        parts = join_cores(own, lax.all_gather(other, "veh"))
        parts = swap(parts, ("y", "x", "pair"))
        parts = swap(sum_and_copy(parts, far), "far")
        new = update_rows(
            parts,
            truck_features,
            customer_average_matrix,
            truck_identity_matrix,
            hidden_offset.reshape(1, -1),
            output_projector,
            chips,
        )
        return swap(new, ("y", "x", "pair"))

    split = ("y", "x", "far", "pair")
    placed = (P(split, None), P(split), P(), P(), P(), P(), P(), P())
    return jax.shard_map(
        on_device, mesh=inner, in_specs=placed, out_specs=P("veh", None), check_vma=False
    )
```
